32 devices in a mesh: seq: 8 (over y, x, core), dp: 4 (over z).
Axes of the slice: x: 2, y: 2, z: 4, core: 2. Of those that a mesh axis runs over, the one named last changes fastest.
Arguments:
- query: bfloat16 [4, 1536, 1280], P('dp', 'seq'), may hold values from -52 to 52, as said below
- keys: bfloat16 [4, 1536, 1280], P('dp', 'seq'), may hold values from -6 to 6, as said below
- values: bfloat16 [4, 1536, 1280], P('dp', 'seq'), may hold values from -6 to 6
- attn: bfloat16 [4, 1536, 1280], P('dp', 'seq'), may hold values from -6 to 6
- d_block: bfloat16 [4, 1536, 1280], P('dp', 'seq'), may hold values from -6 to 6
- w_out: bfloat16 [1280, 1280], P('dp'), may hold values from -0.15625 to 0.15625
Outputs:
- d_query: bfloat16 [4, 1536, 1280], P('dp', 'seq')
- d_keys: bfloat16 [4, 1536, 1280], P('dp', 'seq')
- d_values: bfloat16 [4, 1536, 1280], P('dp', 'seq')
- d_weight: float32 [1280, 1280], P('dp')
The draws below stay inside these ranges and needn't reach their ends.
Inputs may be any that keep to these rules, and one draw needn't show every extreme that they name: Some query patches may lie along the sum of two keys of the same video. keys has entries of order one.
All inputs are finite; a program needn't handle non-finite values.
Results may differ from the reference program's by a relative error of at most 0.0058.
Values may be sent and summed in bfloat16 or wider, within the bound.
A program may use at most 64 MiB of HBM per device.

```python
import jax
import jax.numpy as jnp
from jax import lax

HEADS = 16
HEAD_DIM = 80
D = 1280
PATCHES = 1536
VIDEOS = 4


def shared_pair(key):
    shape_all = (VIDEOS, PATCHES, HEADS * HEAD_DIM)
    keys_raw = jnp.clip(jax.random.normal(jax.random.fold_in(key, 101), shape_all, jnp.float32), -6.0, 6.0)
    query_raw = jnp.clip(jax.random.normal(jax.random.fold_in(key, 202), shape_all, jnp.float32), -6.0, 6.0)
    keys_out = keys_raw
    query_out = query_raw
    return (query_out, keys_out)


def draw_query(key, part):
    return shared_pair(key)[0].astype(jnp.bfloat16)


def draw_keys(key, part):
    return shared_pair(key)[1].astype(jnp.bfloat16)


def raised(entries, own_key, source, target, parts, factor):
    owner, partner = [(jnp.arange(entries.shape[axis_at]) // (entries.shape[axis_at] // parts)).reshape([-1 if axis == axis_at else 1 for axis in range(entries.ndim)]) for axis_at in (source, target)]
    chosen = jax.random.permutation(own_key, parts)[partner]
    strong = (owner == chosen) | (owner == (partner + parts // 2) % parts)
    return jnp.where(strong, factor * entries, entries)


def block_scale(rng, shape, shards, low, top_value):
    gain, own = 1.0, jax.random.fold_in(rng, 6)
    for position, shards_of in shards:
        steps = jnp.exp(jax.random.uniform(jax.random.fold_in(own, position), (shards_of,), jnp.float32, low / len(shards), top_value / len(shards)))
        gain = gain * jnp.repeat(steps, shape[position] // shards_of).reshape([-1 if axis == position else 1 for axis in range(len(shape))])
    return gain


def noise(key, shape, deviation, limit, shards=(), kind=jnp.bfloat16):
    values = deviation * jax.random.normal(key, shape, jnp.float32)
    if shards:
        values = values * block_scale(key, shape, shards, -0.22, 0.18)
    return jnp.clip(values, -limit, limit).astype(kind)


def noise_with(rng, extent, width, reach, shards, heavy, held_as=jnp.bfloat16):
    drawn = width * jax.random.normal(rng, extent, jnp.float32)
    if shards:
        drawn = drawn * block_scale(rng, extent, shards, -0.22, 0.18)
    return jnp.clip(raised(drawn, jax.random.fold_in(rng, 3), *heavy), -reach, reach).astype(held_as)


def setup_inputs(seed: int = 0) -> dict:
    seeds = jax.random.split(jax.random.key(seed), 7)
    query = draw_query(jax.random.fold_in(seeds[6], 71), 0)
    keys = draw_keys(jax.random.fold_in(seeds[6], 71), 0)
    values = noise(seeds[2], (VIDEOS, PATCHES, D), 1.0, 6.0, ((0, 4), (1, 8)))
    attn = noise_with(seeds[3], (VIDEOS, PATCHES, D), 1.0, 6.0, ((0, 4), (1, 8)), (1, 2, 8, 2.0))
    d_block = noise(seeds[4], (VIDEOS, PATCHES, D), 1.0, 6.0, ((0, 4), (1, 8)))
    w_out = noise(seeds[5], (D, D), D ** -0.5, 0.15625, ((0, 4),))
    return dict(query=query, keys=keys, values=values, attn=attn, d_block=d_block, w_out=w_out)


def head_gradients(item):
    query_h, keys_h, values_h, dout_h, delta_h = item
    score_scale = HEAD_DIM ** -0.5
    scores = jnp.dot(query_h, keys_h.T, preferred_element_type=jnp.float32) * score_scale
    row_max = jnp.max(scores, axis=1, keepdims=True)
    lse = row_max + jnp.log(jnp.sum(jnp.exp(scores - row_max), axis=1, keepdims=True))
    probs = jnp.exp(scores - lse)
    probs_low = probs.astype(jnp.bfloat16)
    d_values = jnp.dot(probs_low.T, dout_h, preferred_element_type=jnp.float32)
    d_probs = jnp.dot(dout_h, values_h.T, preferred_element_type=jnp.float32)
    d_scores = (score_scale * probs * (d_probs - delta_h[:, None])).astype(jnp.bfloat16)
    d_query = jnp.dot(d_scores, keys_h, preferred_element_type=jnp.float32)
    d_keys = jnp.dot(d_scores.T, query_h, preferred_element_type=jnp.float32)
    return (d_query.astype(jnp.bfloat16), d_keys.astype(jnp.bfloat16), d_values.astype(jnp.bfloat16))


def reference(query, keys, values, attn, d_block, w_out):
    features = HEADS * HEAD_DIM
    grad_y = d_block.reshape(VIDEOS * PATCHES, features)
    attn_rows = attn.reshape(VIDEOS * PATCHES, features)
    d_out = jnp.dot(grad_y, w_out.T, preferred_element_type=jnp.float32).astype(jnp.bfloat16)
    delta = jnp.sum((d_out.astype(jnp.float32) * attn_rows.astype(jnp.float32)).reshape(VIDEOS, PATCHES, HEADS, HEAD_DIM), axis=3)

    def by_head(array):
        return array.reshape(VIDEOS, PATCHES, HEADS, HEAD_DIM).transpose(0, 2, 1, 3).reshape(VIDEOS * HEADS, PATCHES, HEAD_DIM)

    delta_heads = delta.transpose(0, 2, 1).reshape(VIDEOS * HEADS, PATCHES)
    d_query, d_keys, d_values = lax.map(head_gradients, (by_head(query), by_head(keys), by_head(values), by_head(d_out.reshape(VIDEOS, PATCHES, features)), delta_heads))

    def by_patch(array):
        return array.reshape(VIDEOS, HEADS, PATCHES, HEAD_DIM).transpose(0, 2, 1, 3).reshape(VIDEOS, PATCHES, features)

    total = jnp.dot(attn_rows.T, grad_y, preferred_element_type=jnp.float32)
    d_weight = total * (1.0 / (float(VIDEOS * PATCHES) ** 0.5))
    return (by_patch(d_query), by_patch(d_keys), by_patch(d_values), d_weight)
```

```python
import functools
import math

import jax
import jax.numpy as jnp
from jax import lax
from jax.experimental import pallas as pl
from jax.experimental.pallas import tpu as pltpu
from jax.sharding import PartitionSpec as P

HEAD_DIM = 80
AUG = HEAD_DIM + 8
MESH = pl.DeviceIdType.MESH
VMEM_LIMIT = 62 * 1024 * 1024
LAST = (((1,), (1,)), ((), ()))
FIRST = (((0,), (0,)), ((), ()))
BF16 = jnp.bfloat16
F32 = jnp.float32


def attention_kernel(
    seq, dp, heads, block, factor,
    q_hbm, k_hbm, v_hbm, a_hbm, g_hbm, w_hbm, landed, spread,
    q_v, k_v, v_v, g_v, a2, g2, w_all, packed, pack_in, do_out, do_in,
    q_s, k_s, v_s, qs_s, dos_s, e_s, inv_s, dqt_s, grad_s,
    p_s, up_out, up_in, dn_out, dn_in, acc_s, rs_out, rs_in, total_s,
    in_sem, own_sem, wu_send, wd_send, wp_send, w_recv, x_send, x_recv,
    q_send, q_recv, do_send, do_recv, g_send, g_recv,
    up_send, up_recv, dn_send, dn_recv, rs_send, rs_recv, t_send, f_send, t_recv,
):
    s = lax.axis_index("seq")
    d = lax.axis_index("dp")
    core = s % 2
    chip = s // 2
    chips = seq // 2
    partner = s + 1 - 2 * core
    ratio = seq // dp
    rows, features = q_v.shape
    half = features // 2
    width = heads * HEAD_DIM
    patches = seq * rows
    slab = features // dp
    share = slab // chips
    blocks = patches // block
    scale = HEAD_DIM ** (-0.5)
    to_log2 = scale * math.log2(math.e)

    def columns(which):
        return pl.ds(pl.multiple_of(which * half, 128), half)

    def remote(src, dst, send, recv, peer, plane):
        return pltpu.make_async_remote_copy(
            src_ref=src, dst_ref=dst, send_sem=send, recv_sem=recv,
            device_id=(peer, plane), device_id_type=MESH,
        )

    barrier = pltpu.get_barrier_semaphore()
    for step in range(1, seq):
        pl.semaphore_signal(barrier, inc=1, device_id=(lax.rem(s + step, seq), d), device_id_type=MESH)
    for step in range(1, dp):
        pl.semaphore_signal(barrier, inc=1, device_id=(s, lax.rem(d + step, dp)), device_id_type=MESH)

    loads = [
        pltpu.make_async_copy(src, dst, in_sem.at[index])
        for index, (src, dst) in enumerate((
            (q_hbm, q_v), (k_hbm, k_v), (v_hbm, v_v), (a_hbm, a2.at[0]), (g_hbm, g_v),
            (g_hbm.at[:, columns(core)], g2.at[0]),
        ))
    ]
    own_w = [
        pltpu.make_async_copy(
            w_hbm.at[:, h], w_all.at[h, pl.ds(d * ratio, ratio)], in_sem.at[6 + h]
        )
        for h in range(heads)
    ]
    for copy in loads + own_w:
        copy.start()

    def w_piece(h, b, which):
        return w_all.at[h, pl.ds(b * ratio, ratio), :, columns(which)]

    def w_up(h, b, own):
        src = w_hbm.at[:, h, :, columns(core)] if own else w_piece(h, b, core)
        return remote(src, w_piece(h, b, core), wu_send.at[h, b], w_recv.at[h, b, core], s, d + 1)

    def w_down(h, b, own):
        src = w_hbm.at[:, h, :, columns(core)] if own else w_piece(h, b, core)
        return remote(src, w_piece(h, b, core), wd_send.at[h, b], w_recv.at[h, b, core], s, d - 1)

    def w_side(h, b, which):
        return remote(
            w_piece(h, b, which), w_piece(h, b, which), wp_send.at[h, b], w_recv.at[h, b, which], partner, d
        )

    def w_own(h):
        pl.when(d < dp - 1)(lambda: w_up(h, d, True).start())
        pl.when(d > 0)(lambda: w_down(h, d, True).start())

    def w_relay(h, dist):
        @pl.when(d >= dist)
        def _():
            b = d - dist
            w_side(h, b, core).wait_recv()
            pl.when(d < dp - 1)(lambda: w_up(h, b, False).start())
            w_side(h, b, core).start()

        @pl.when(d + dist < dp)
        def _():
            b = d + dist
            w_side(h, b, core).wait_recv()
            pl.when(d > 0)(lambda: w_down(h, b, False).start())
            w_side(h, b, core).start()

    def w_finish(h):
        for dist in range(1, dp):
            pl.when(d >= dist)(lambda: w_side(h, d - dist, 1 - core).wait_recv())
            pl.when(d + dist < dp)(lambda: w_side(h, d + dist, 1 - core).wait_recv())
        own_w[h].wait()

    def w_drain(h):
        pl.when(d < dp - 1)(lambda: w_up(h, d, True).wait_send())
        pl.when(d > 0)(lambda: w_down(h, d, True).wait_send())
        for dist in range(1, dp):
            @pl.when(d >= dist)
            def _():
                pl.when(d < dp - 1)(lambda: w_up(h, d - dist, False).wait_send())
                w_side(h, d - dist, core).wait_send()

            @pl.when(d + dist < dp)
            def _():
                pl.when(d > 0)(lambda: w_down(h, d + dist, False).wait_send())
                w_side(h, d + dist, core).wait_send()

    def q_copy(h, peer, source):
        return remote(packed.at[h, peer], pack_in.at[h, source], q_send.at[h, peer], q_recv.at[h, source], peer, d)

    def do_copy(h, peer, source):
        return remote(do_out.at[h, peer], do_in.at[h, source], do_send.at[h, peer], do_recv.at[h, source], peer, d)

    def grad_copy(h, peer, source):
        start = pl.multiple_of(peer * rows, rows)
        return remote(
            grad_s.at[h, pl.ds(start, rows)], landed.at[h, source], g_send.at[h, peer], g_recv.at[h, source], peer, d
        )

    def own_q(h):
        return pltpu.make_async_copy(packed.at[h, s], pack_in.at[h, s], own_sem.at[0, h])

    def own_do(h):
        return pltpu.make_async_copy(do_out.at[h, s], do_in.at[h, s], own_sem.at[1, h])

    def own_grad(h):
        start = pl.multiple_of(s * rows, rows)
        return pltpu.make_async_copy(grad_s.at[h, pl.ds(start, rows)], landed.at[h, s], own_sem.at[2, h])

    def send_all(copy, own, h):
        for step in range(1, seq):
            copy(h, lax.rem(s + step, seq), s).start()
        own(h).start()

    def await_all(copy, own, h):
        own(h).wait()
        for step in range(1, seq):
            source = lax.rem(s + seq - step, seq)
            copy(h, source, source).wait_recv()

    def drain_all(copy, h):
        for step in range(1, seq):
            copy(h, lax.rem(s + step, seq), s).wait_send()

    def pack(h):
        for peer in range(seq):
            low = peer * width + h * HEAD_DIM
            for index, ref in enumerate((q_v, k_v, v_v)):
                packed[h, peer, :, index * HEAD_DIM : (index + 1) * HEAD_DIM] = ref[:, low : low + HEAD_DIM]

    def make_d_out(h):
        d_out = lax.dot_general(
            g_v[...], w_all[h].reshape(seq * HEAD_DIM, features), LAST, preferred_element_type=F32
        ).astype(BF16)
        lane = lax.broadcasted_iota(jnp.int32, (rows, AUG - HEAD_DIM), 1)
        for peer in range(seq):
            low = peer * width + h * HEAD_DIM
            piece = d_out[:, peer * HEAD_DIM : (peer + 1) * HEAD_DIM]
            product = piece.astype(F32) * a2[0, :, low : low + HEAD_DIM].astype(F32)
            minus = -jnp.sum(product, axis=1, keepdims=True)
            first = minus.astype(BF16).astype(F32)
            second = (minus - first).astype(BF16).astype(F32)
            third = minus - first - second
            tail = jnp.where(lane == 0, first, jnp.where(lane == 1, second, jnp.where(lane == 2, third, 0.0)))
            do_out[h, peer, :, 0:HEAD_DIM] = piece
            do_out[h, peer, :, HEAD_DIM:AUG] = tail.astype(BF16)

    def a_swap():
        return remote(a_hbm, a2.at[1], x_send.at[0], x_recv.at[0], partner, d)

    def g_swap():
        return remote(g_hbm.at[:, columns(1 - core)], g2.at[1], x_send.at[1], x_recv.at[1], partner, d)

    def slab_rows(b):
        return pl.ds(pl.multiple_of(b * slab, slab), slab)

    def up_copy(k):
        return remote(up_out.at[k], up_in.at[k], up_send.at[k], up_recv.at[k], s, d + 1)

    def dn_copy(k):
        return remote(dn_out.at[k], dn_in.at[k], dn_send.at[k], dn_recv.at[k], s, d - 1)

    def chain(k):
        back = dp - 1 - d

        @pl.when(d <= k)
        def _():
            b = dp - 1 - k + d

            @pl.when(d == 0)
            def _():
                up_out[k] = p_s[slab_rows(b), :].astype(BF16)

            if k:
                @pl.when(d > 0)
                def _():
                    up_copy(k - 1).wait_recv()
                    up_out[k] = (p_s[slab_rows(b), :] + up_in[k - 1].astype(F32)).astype(BF16)

            up_copy(k).start()

        @pl.when(back <= k)
        def _():
            b = k - back

            @pl.when(back == 0)
            def _():
                dn_out[k] = p_s[slab_rows(b), :].astype(BF16)

            if k:
                @pl.when(back > 0)
                def _():
                    dn_copy(k - 1).wait_recv()
                    dn_out[k] = (p_s[slab_rows(b), :] + dn_in[k - 1].astype(F32)).astype(BF16)

            dn_copy(k).start()

    def chain_drain():
        for k in range(dp - 1):
            pl.when(d <= k)(lambda: up_copy(k).wait_send())
            pl.when(dp - 1 - d <= k)(lambda: dn_copy(k).wait_send())

    def rs_copy(target, source):
        return remote(rs_out.at[target], rs_in.at[source], rs_send.at[target], rs_recv.at[source], 2 * target + core, d)

    def scatter():
        acc_s[...] = p_s[slab_rows(d), :]

        @pl.when(d > 0)
        def _():
            up_copy(dp - 2).wait_recv()
            acc_s[...] += up_in[dp - 2].astype(F32)

        @pl.when(d < dp - 1)
        def _():
            dn_copy(dp - 2).wait_recv()
            acc_s[...] += dn_in[dp - 2].astype(F32)

        for index in range(chips):
            rs_out[index] = acc_s[index * share : (index + 1) * share, :].astype(BF16)
        for step in range(1, chips):
            rs_copy(lax.rem(chip + step, chips), chip).start()

    def direct(step):
        return remote(total_s, spread.at[s], t_send.at[step], t_recv.at[s], lax.rem(s + 2 * step, seq), d)

    def forward(step):
        source = lax.rem(s + seq - 2 * step, seq)
        return remote(
            total_s if step == 0 else spread.at[source], spread.at[source],
            f_send.at[step], t_recv.at[source], partner, d,
        )

    def arrived(source):
        remote(total_s, spread.at[source], f_send.at[0], t_recv.at[source], partner, d).wait_recv()

    own_total = pltpu.make_async_copy(total_s, spread.at[s], own_sem.at[3, 0])

    def combine():
        value = rs_out[chip].astype(F32)
        for step in range(1, chips):
            source = lax.rem(chip + chips - step, chips)
            rs_copy(source, source).wait_recv()
            value = value + rs_in[source].astype(F32)
        total_s[...] = value.astype(BF16)
        for step in range(1, chips):
            direct(step).start()
        forward(0).start()
        own_total.start()

    def soften(h, index):
        cut = slice(index * block, (index + 1) * block)
        scores = lax.dot_general(k_s[h], q_s[h, cut, :], LAST, preferred_element_type=F32)
        top = jnp.max(scores, axis=0, keepdims=True)
        exps = jnp.exp2((scores - top) * to_log2)
        inv_s[h, :, cut] = 1.0 / jnp.sum(exps, axis=0, keepdims=True)
        e_s[h, :, cut] = exps.astype(BF16)

    def unpack(h):
        await_all(q_copy, own_q, h)
        for source in range(seq):
            cut = slice(source * rows, (source + 1) * rows)
            q_s[h, cut, :] = pack_in[h, source, :, 0:HEAD_DIM]
            k_s[h, cut, :] = pack_in[h, source, :, HEAD_DIM : 2 * HEAD_DIM]
            v_s[h, cut, 0:HEAD_DIM] = pack_in[h, source, :, 2 * HEAD_DIM : 3 * HEAD_DIM]
            v_s[h, cut, HEAD_DIM:AUG] = jnp.ones((rows, AUG - HEAD_DIM), BF16)

    def prepare(h):
        await_all(do_copy, own_do, h)
        for index in range(blocks):
            cut = slice(index * block, (index + 1) * block)
            column = jnp.broadcast_to(inv_s[h, :, cut], (8, block)).T[:, 0:1]
            qs_s[cut, :] = (q_s[h, cut, :].astype(F32) * (column * scale)).astype(BF16)
        for source in range(seq):
            cut = slice(source * rows, (source + 1) * rows)
            dos_s[cut, :] = do_in[h, source]
        dqt_s[...] = jnp.zeros_like(dqt_s)

    def differentiate(h, index):
        cut = slice(index * block, (index + 1) * block)
        d_out = dos_s[...]
        exps = e_s[h, cut, :]
        inverse = inv_s[h]
        d_probs = lax.dot_general(v_s[h, cut, :], d_out, LAST, preferred_element_type=F32)
        d_scores = (exps.astype(F32) * d_probs).astype(BF16)
        probs = (exps.astype(F32) * inverse).astype(BF16)
        d_v = jnp.dot(probs, d_out, preferred_element_type=F32)
        d_k = jnp.dot(d_scores, qs_s[...], preferred_element_type=F32)
        dqt_s[...] += lax.dot_general(k_s[h, cut, :], d_scores, FIRST, preferred_element_type=F32)
        grad_s[h, cut, HEAD_DIM : 2 * HEAD_DIM] = d_k.astype(BF16)
        grad_s[h, cut, 2 * HEAD_DIM : 3 * HEAD_DIM] = d_v[:, 0:HEAD_DIM].astype(BF16)

    def finish(h):
        grad_s[h, :, 0:HEAD_DIM] = (dqt_s[...] * (inv_s[h] * scale)).T.astype(BF16)
        send_all(grad_copy, own_grad, h)

    pl.semaphore_wait(barrier, seq + dp - 2)
    w_own(0)
    a_swap().start()
    g_swap().start()
    for copy in loads[:3]:
        copy.wait()
    for h in range(heads):
        pack(h)
        send_all(q_copy, own_q, h)
    for copy in loads[3:]:
        copy.wait()
    a_swap().wait_recv()
    g_swap().wait_recv()
    p_s[...] = factor * lax.dot_general(
        a2[...].reshape(2 * rows, features), g2[...].reshape(2 * rows, half), FIRST, preferred_element_type=F32
    )
    w_relay(0, 1)
    for h in range(1, heads):
        w_own(h)
    chain(0)

    links = 1
    for h in range(heads):
        unpack(h)
        for index in range(blocks):
            soften(h, index)
            if h == 0 and index == 0:
                for dist in range(2, dp - 1):
                    w_relay(0, dist)
            if h == 0 and index == blocks - 1:
                if dp > 2:
                    w_relay(0, dp - 1)
                w_finish(0)
                make_d_out(0)
                send_all(do_copy, own_do, 0)
                for g in range(1, heads):
                    w_relay(g, 1)
            if h == 1 and index == 0:
                for g in range(1, heads):
                    for dist in range(2, dp - 1):
                        w_relay(g, dist)
                if links < dp - 1:
                    chain(links)
                    links += 1

    for h in range(heads):
        prepare(h)
        for index in range(blocks):
            differentiate(h, index)
            if h == 0 and index == 0:
                for g in range(1, heads):
                    if dp > 2:
                        w_relay(g, dp - 1)
                    w_finish(g)
                    make_d_out(g)
                    send_all(do_copy, own_do, g)
        finish(h)
        if h == 0:
            while links < dp - 1:
                chain(links)
                links += 1

    scatter()
    combine()
    for step in range(1, chips):
        arrived(lax.rem(s + seq - 2 * step, seq))
        forward(step).start()
    for h in range(heads):
        await_all(grad_copy, own_grad, h)
    for step in range(chips):
        arrived(lax.rem(partner + seq - 2 * step, seq))
    own_total.wait()

    for h in range(heads):
        w_drain(h)
        drain_all(q_copy, h)
        drain_all(do_copy, h)
        drain_all(grad_copy, h)
    a_swap().wait_send()
    g_swap().wait_send()
    chain_drain()
    for step in range(1, chips):
        rs_copy(lax.rem(chip + step, chips), chip).wait_send()
        direct(step).wait_send()
    for step in range(chips):
        forward(step).wait_send()


def attention(seq, dp, factor, query, keys, values, attn, grad_y, w_rows):
    rows, features = query.shape
    heads = w_rows.shape[1]
    ratio = w_rows.shape[0]
    total = seq * rows
    half = features // 2
    slab = features // dp
    chips = seq // 2
    share = slab // chips
    block = 768
    while total % block or total * block > 1536 * 768:
        block //= 2
    dma = pltpu.SemaphoreType.DMA
    hbm = pl.BlockSpec(memory_space=pl.ANY)
    low = lambda *shape: pltpu.VMEM(shape, BF16)
    wide = lambda *shape: pltpu.VMEM(shape, F32)
    links = max(dp - 1, 1)
    return pl.pallas_call(
        functools.partial(attention_kernel, seq, dp, heads, block, factor),
        out_shape=(
            jax.ShapeDtypeStruct((heads, seq, rows, 3 * HEAD_DIM), BF16),
            jax.ShapeDtypeStruct((seq, share, half), BF16),
        ),
        in_specs=[hbm] * 6,
        out_specs=(hbm, hbm),
        scratch_shapes=[
            low(rows, features), low(rows, features), low(rows, features), low(rows, features),
            low(2, rows, features), low(2, rows, half),
            low(heads, seq, HEAD_DIM, features),
            low(heads, seq, rows, 3 * HEAD_DIM), low(heads, seq, rows, 3 * HEAD_DIM),
            low(heads, seq, rows, AUG), low(heads, seq, rows, AUG),
            low(heads, total, HEAD_DIM), low(heads, total, HEAD_DIM), low(heads, total, AUG),
            low(total, HEAD_DIM), low(total, AUG),
            low(heads, total, total), wide(heads, 1, total),
            wide(HEAD_DIM, total), low(heads, total, 3 * HEAD_DIM),
            wide(features, half),
            low(links, slab, half), low(links, slab, half), low(links, slab, half), low(links, slab, half),
            wide(slab, half), low(chips, share, half), low(chips, share, half), low(share, half),
            dma((6 + heads,)), dma((4, heads)),
            dma((heads, dp)), dma((heads, dp)), dma((heads, dp)), dma((heads, dp, 2)),
            dma((2,)), dma((2,)),
            dma((heads, seq)), dma((heads, seq)), dma((heads, seq)), dma((heads, seq)),
            dma((heads, seq)), dma((heads, seq)),
            dma((links,)), dma((links,)), dma((links,)), dma((links,)),
            dma((chips,)), dma((chips,)), dma((chips,)), dma((chips,)), dma((seq,)),
        ],
        compiler_params=pltpu.CompilerParams(
            collective_id=0, has_side_effects=True, vmem_limit_bytes=VMEM_LIMIT
        ),
        name="attention_backward",
    )(query, keys, values, attn, grad_y, w_rows)


def unpack_kernel(landed, spread, dq_ref, dk_ref, dv_ref, out_ref):
    heads, seq = landed.shape[:2]
    share, half = spread.shape[1:]
    width = heads * HEAD_DIM
    for source in range(seq):
        for h in range(heads):
            start = source * width + h * HEAD_DIM
            for index, ref in enumerate((dq_ref, dk_ref, dv_ref)):
                ref[:, start : start + HEAD_DIM] = landed[
                    h, source, :, index * HEAD_DIM : (index + 1) * HEAD_DIM
                ]
        top = (source // 2) * share
        side = (source % 2) * half
        out_ref[top : top + share, side : side + half] = spread[source].astype(F32)


def unpack(dp, landed, spread):
    rows = landed.shape[2]
    features = landed.shape[0] * landed.shape[1] * HEAD_DIM
    vmem = pl.BlockSpec(memory_space=pltpu.VMEM)
    block = jax.ShapeDtypeStruct((rows, features), BF16)
    return pl.pallas_call(
        unpack_kernel,
        out_shape=(block, block, block, jax.ShapeDtypeStruct((features // dp, features), F32)),
        in_specs=[vmem] * 2,
        out_specs=(vmem,) * 4,
        compiler_params=pltpu.CompilerParams(vmem_limit_bytes=VMEM_LIMIT),
        name="unpack",
    )(landed, spread)


def body(query, keys, values, attn, d_block, w_out):
    seq = lax.axis_size("seq")
    dp = lax.axis_size("dp")
    rows, features = query.shape[1:]
    heads = features // HEAD_DIM // seq
    flat = lambda array: array.reshape(rows, features)
    factor = 1.0 / float(dp * rows * seq) ** 0.5
    landed, spread = attention(
        seq, dp, factor, flat(query), flat(keys), flat(values), flat(attn), flat(d_block),
        w_out.reshape(seq // dp, heads, HEAD_DIM, features),
    )
    d_query, d_keys, d_values, d_weight = unpack(dp, landed, spread)
    whole = lambda array: array.reshape(1, rows, features)
    return whole(d_query), whole(d_keys), whole(d_values), d_weight


def solution(mesh):
    blocks = P("dp", "seq", None)
    return jax.shard_map(
        body,
        mesh=mesh,
        in_specs=(blocks,) * 5 + (P("dp", None),),
        out_specs=(blocks, blocks, blocks, P("dp", None)),
        check_vma=False,
    )
```

```python
import functools
import math

import jax
import jax.numpy as jnp
from jax import lax
from jax.experimental import pallas as pl
from jax.experimental.pallas import tpu as pltpu
from jax.sharding import PartitionSpec as P

HEAD_DIM = 80
AUG = HEAD_DIM + 3
FOLD = 3
PIECES = 2
MESH = pl.DeviceIdType.MESH
VMEM_LIMIT = 62 * 1024 * 1024
LAST = (((1,), (1,)), ((), ()))
FIRST = (((0,), (0,)), ((), ()))
BF16 = jnp.bfloat16
F32 = jnp.float32


def attention_kernel(
    seq, dp, heads, block, factor,
    q_hbm, k_hbm, v_hbm, a_hbm, g_hbm, w_hbm, landed, spread,
    q_v, k_v, v_v, g_v, a2, g2, w_all, packed, pack_in, a_s, do_out, do_in,
    q_s, k_s, v_s, qs_s, dos_s, e_s, inv_s, dqt_s, grad_s,
    p_s, up_out, up_in, dn_out, dn_in, acc_s, rs_out, rs_in, total_s,
    in_sem, own_sem, wu_send, wd_send, wp_send, w_recv, x_send, x_recv,
    q_send, q_recv, do_send, do_recv, g_send, g_recv,
    up_send, up_recv, dn_send, dn_recv, rs_send, rs_recv, t_send, f_send, t_recv,
):
    s = lax.axis_index("seq")
    d = lax.axis_index("dp")
    core = s % 2
    chip = s // 2
    chips = seq // 2
    partner = s + 1 - 2 * core
    ratio = seq // dp
    rows, features = q_v.shape
    half = features // 2
    width = heads * HEAD_DIM
    patches = seq * rows
    slab = features // dp
    share = slab // chips
    blocks = patches // block
    scale = HEAD_DIM ** (-0.5)
    to_log2 = scale * math.log2(math.e)

    def columns(which):
        return pl.ds(pl.multiple_of(which * half, 128), half)

    def remote(src, dst, send, recv, peer, plane):
        return pltpu.make_async_remote_copy(
            src_ref=src, dst_ref=dst, send_sem=send, recv_sem=recv,
            device_id=(peer, plane), device_id_type=MESH,
        )

    barrier = pltpu.get_barrier_semaphore()
    for step in range(1, seq):
        pl.semaphore_signal(barrier, inc=1, device_id=(lax.rem(s + step, seq), d), device_id_type=MESH)
    for step in range(1, dp):
        pl.semaphore_signal(barrier, inc=1, device_id=(s, lax.rem(d + step, dp)), device_id_type=MESH)

    loads = [
        pltpu.make_async_copy(src, dst, in_sem.at[index])
        for index, (src, dst) in enumerate((
            (q_hbm, q_v), (k_hbm, k_v), (v_hbm, v_v), (a_hbm, a2.at[0]), (g_hbm, g_v),
            (g_hbm.at[:, columns(core)], g2.at[0]),
        ))
    ]
    own_w = [
        pltpu.make_async_copy(
            w_hbm.at[:, h], w_all.at[h, pl.ds(d * ratio, ratio)], in_sem.at[6 + h]
        )
        for h in range(heads)
    ]
    for copy in loads + own_w:
        copy.start()

    def w_piece(h, b, which):
        return w_all.at[h, pl.ds(b * ratio, ratio), :, columns(which)]

    def w_up(h, b, own):
        src = w_hbm.at[:, h, :, columns(core)] if own else w_piece(h, b, core)
        return remote(src, w_piece(h, b, core), wu_send.at[h, b], w_recv.at[h, b, core], s, d + 1)

    def w_down(h, b, own):
        src = w_hbm.at[:, h, :, columns(core)] if own else w_piece(h, b, core)
        return remote(src, w_piece(h, b, core), wd_send.at[h, b], w_recv.at[h, b, core], s, d - 1)

    def w_side(h, b, which):
        return remote(
            w_piece(h, b, which), w_piece(h, b, which), wp_send.at[h, b], w_recv.at[h, b, which], partner, d
        )

    def w_own(h):
        pl.when(d < dp - 1)(lambda: w_up(h, d, True).start())
        pl.when(d > 0)(lambda: w_down(h, d, True).start())

    def w_ends(h):
        pl.when(d == 0)(lambda: w_up(h, d, True).start())
        pl.when(d == dp - 1)(lambda: w_down(h, d, True).start())

    def w_inner(h):
        @pl.when((d > 0) & (d < dp - 1))
        def _():
            w_up(h, d, True).start()
            w_down(h, d, True).start()

    def w_relay(h, dist):
        @pl.when(d >= dist)
        def _():
            b = d - dist
            w_side(h, b, core).wait_recv()
            pl.when(d < dp - 1)(lambda: w_up(h, b, False).start())
            w_side(h, b, core).start()

        @pl.when(d + dist < dp)
        def _():
            b = d + dist
            w_side(h, b, core).wait_recv()
            pl.when(d > 0)(lambda: w_down(h, b, False).start())
            w_side(h, b, core).start()

    def w_drain(h):
        pl.when(d < dp - 1)(lambda: w_up(h, d, True).wait_send())
        pl.when(d > 0)(lambda: w_down(h, d, True).wait_send())
        for dist in range(1, dp):
            @pl.when(d >= dist)
            def _():
                pl.when(d < dp - 1)(lambda: w_up(h, d - dist, False).wait_send())
                w_side(h, d - dist, core).wait_send()

            @pl.when(d + dist < dp)
            def _():
                pl.when(d > 0)(lambda: w_down(h, d + dist, False).wait_send())
                w_side(h, d + dist, core).wait_send()

    def q_copy(h, peer, source):
        return remote(packed.at[h, peer], pack_in.at[h, source], q_send.at[h, peer], q_recv.at[h, source], peer, d)

    def do_copy(h, peer, source):
        return remote(do_out.at[h, peer], do_in.at[h, source], do_send.at[h, peer], do_recv.at[h, source], peer, d)

    def grad_copy(h, peer, source):
        start = pl.multiple_of(peer * rows, rows)
        return remote(
            grad_s.at[h, pl.ds(start, rows)], landed.at[h, source], g_send.at[h, peer], g_recv.at[h, source], peer, d
        )

    def own_q(h):
        return pltpu.make_async_copy(packed.at[h, s], pack_in.at[h, s], own_sem.at[0, h])

    def own_do(h):
        return pltpu.make_async_copy(do_out.at[h, s], do_in.at[h, s], own_sem.at[1, h])

    def own_grad(h):
        start = pl.multiple_of(s * rows, rows)
        return pltpu.make_async_copy(grad_s.at[h, pl.ds(start, rows)], landed.at[h, s], own_sem.at[2, h])

    def send_all(copy, own, h):
        for step in range(1, seq):
            copy(h, lax.rem(s + step, seq), s).start()
        own(h).start()

    def await_all(copy, own, h):
        own(h).wait()
        for step in range(1, seq):
            source = lax.rem(s + seq - step, seq)
            copy(h, source, source).wait_recv()

    def drain_all(copy, h):
        for step in range(1, seq):
            copy(h, lax.rem(s + step, seq), s).wait_send()

    def pack(h):
        for peer in range(seq):
            low = peer * width + h * HEAD_DIM
            for index, ref in enumerate((q_v, k_v, v_v)):
                packed[h, peer, :, index * HEAD_DIM : (index + 1) * HEAD_DIM] = ref[:, low : low + HEAD_DIM]

    def pack_attn(h):
        for peer in range(seq):
            low = peer * width + h * HEAD_DIM
            a_s[h, peer] = a2[0, :, low : low + HEAD_DIM]

    def make_d_out(h, b):
        d_out = lax.dot_general(
            g_v[...], w_all[h, pl.ds(b * ratio, ratio)].reshape(ratio * HEAD_DIM, features), LAST,
            preferred_element_type=F32,
        ).astype(BF16)
        lane = lax.broadcasted_iota(jnp.int32, (rows, AUG - HEAD_DIM), 1)
        fold = rows // FOLD
        for member in range(ratio):
            peer = b * ratio + member
            piece = d_out[:, member * HEAD_DIM : (member + 1) * HEAD_DIM]
            product = piece.astype(F32) * a_s[h, peer].astype(F32)
            minus = -jnp.sum(product, axis=1, keepdims=True)
            first = minus.astype(BF16).astype(F32)
            second = (minus - first).astype(BF16).astype(F32)
            third = minus - first - second
            tail = jnp.where(lane == 0, first, jnp.where(lane == 1, second, third)).astype(BF16)
            for index in range(FOLD):
                cut = slice(index * fold, (index + 1) * fold)
                do_out[h, peer, :, index * AUG : index * AUG + HEAD_DIM] = piece[cut]
                do_out[h, peer, :, index * AUG + HEAD_DIM : (index + 1) * AUG] = tail[cut]
        for member in range(ratio):
            peer = b * ratio + member
            pl.when(peer != s)(lambda: do_copy(h, peer, s).start())
            pl.when(peer == s)(lambda: own_do(h).start())

    def d_out_pair(h, dist):
        @pl.loop(0, 2)
        def _(side):
            b = d + (2 * side - 1) * dist

            @pl.when((b >= 0) & (b < dp))
            def _():
                w_side(h, b, 1 - core).wait_recv()
                make_d_out(h, b)

    def a_swap():
        return remote(a_hbm, a2.at[1], x_send.at[0], x_recv.at[0], partner, d)

    def g_swap():
        return remote(g_hbm.at[:, columns(1 - core)], g2.at[1], x_send.at[1], x_recv.at[1], partner, d)

    def slab_rows(b, j):
        return pl.ds(pl.multiple_of(b * slab + j * (slab // PIECES), 8), slab // PIECES)

    def up_copy(k, j):
        return remote(up_out.at[k, j], up_in.at[k, j], up_send.at[k, j], up_recv.at[k, j], s, d + 1)

    def dn_copy(k, j):
        return remote(dn_out.at[k, j], dn_in.at[k, j], dn_send.at[k, j], dn_recv.at[k, j], s, d - 1)

    back = dp - 1 - d

    def chain_ends():
        @pl.when(d == 0)
        def _():
            for k in range(dp - 1):
                for j in range(PIECES):
                    up_out[k, j] = p_s[slab_rows(dp - 1 - k, j), :].astype(BF16)
                    up_copy(k, j).start()

        @pl.when(back == 0)
        def _():
            for k in range(dp - 1):
                for j in range(PIECES):
                    dn_out[k, j] = p_s[slab_rows(k, j), :].astype(BF16)
                    dn_copy(k, j).start()

    def chain(k, j):
        @pl.when((d > 0) & (d <= k))
        def _():
            up_copy(k - 1, j).wait_recv()
            up_out[k, j] = (p_s[slab_rows(dp - 1 - k + d, j), :] + up_in[k - 1, j].astype(F32)).astype(BF16)
            up_copy(k, j).start()

        @pl.when((back > 0) & (back <= k))
        def _():
            dn_copy(k - 1, j).wait_recv()
            dn_out[k, j] = (p_s[slab_rows(k - back, j), :] + dn_in[k - 1, j].astype(F32)).astype(BF16)
            dn_copy(k, j).start()

    def chain_drain():
        for k in range(dp - 1):
            for j in range(PIECES):
                pl.when(d <= k)(lambda: up_copy(k, j).wait_send())
                pl.when(back <= k)(lambda: dn_copy(k, j).wait_send())

    def rs_copy(target, source):
        return remote(rs_out.at[target], rs_in.at[source], rs_send.at[target], rs_recv.at[source], 2 * target + core, d)

    def scatter():
        tall = slab // PIECES
        for j in range(PIECES):
            cut = slice(j * tall, (j + 1) * tall)
            acc_s[cut, :] = p_s[slab_rows(d, j), :]

            @pl.when(d > 0)
            def _():
                up_copy(dp - 2, j).wait_recv()
                acc_s[cut, :] += up_in[dp - 2, j].astype(F32)

            @pl.when(d < dp - 1)
            def _():
                dn_copy(dp - 2, j).wait_recv()
                acc_s[cut, :] += dn_in[dp - 2, j].astype(F32)

        for index in range(chips):
            rs_out[index] = acc_s[index * share : (index + 1) * share, :].astype(BF16)
        for step in range(1, chips):
            rs_copy(lax.rem(chip + step, chips), chip).start()

    def direct(step):
        return remote(total_s, spread.at[s], t_send.at[step], t_recv.at[s], lax.rem(s + 2 * step, seq), d)

    def forward(step):
        source = lax.rem(s + seq - 2 * step, seq)
        return remote(
            total_s if step == 0 else spread.at[source], spread.at[source],
            f_send.at[step], t_recv.at[source], partner, d,
        )

    def arrived(source):
        remote(total_s, spread.at[source], f_send.at[0], t_recv.at[source], partner, d).wait_recv()

    own_total = pltpu.make_async_copy(total_s, spread.at[s], own_sem.at[3, 0])

    def combine():
        value = rs_out[chip].astype(F32)
        for step in range(1, chips):
            source = lax.rem(chip + chips - step, chips)
            rs_copy(source, source).wait_recv()
            value = value + rs_in[source].astype(F32)
        total_s[...] = value.astype(BF16)
        for step in range(1, chips):
            direct(step).start()
        forward(0).start()
        own_total.start()

    def soften(h, index):
        cut = slice(index * block, (index + 1) * block)
        scores = lax.dot_general(k_s[h], q_s[h, cut, :], LAST, preferred_element_type=F32)
        top = jnp.max(scores, axis=0, keepdims=True)
        exps = jnp.exp2((scores - top) * to_log2)
        inv_s[h, :, cut] = 1.0 / jnp.sum(exps, axis=0, keepdims=True)
        e_s[h, :, cut] = exps.astype(BF16)

    def unpack(h):
        await_all(q_copy, own_q, h)
        for source in range(seq):
            cut = slice(source * rows, (source + 1) * rows)
            q_s[h, cut, :] = pack_in[h, source, :, 0:HEAD_DIM]
            k_s[h, cut, :] = pack_in[h, source, :, HEAD_DIM : 2 * HEAD_DIM]
            v_s[h, cut, 0:HEAD_DIM] = pack_in[h, source, :, 2 * HEAD_DIM : 3 * HEAD_DIM]
            v_s[h, cut, HEAD_DIM:AUG] = jnp.ones((rows, AUG - HEAD_DIM), BF16)

    def prepare(h):
        await_all(do_copy, own_do, h)
        for index in range(blocks):
            cut = slice(index * block, (index + 1) * block)
            column = jnp.broadcast_to(inv_s[h, :, cut], (8, block)).T[:, 0:1]
            qs_s[cut, :] = (q_s[h, cut, :].astype(F32) * (column * scale)).astype(BF16)
        fold = rows // FOLD
        for source in range(seq):
            for index in range(FOLD):
                start = source * rows + index * fold
                dos_s[start : start + fold, :] = do_in[h, source, :, index * AUG : (index + 1) * AUG]
        dqt_s[...] = jnp.zeros_like(dqt_s)

    def differentiate(h, index):
        cut = slice(index * block, (index + 1) * block)
        d_out = dos_s[...]
        exps = e_s[h, cut, :]
        inverse = inv_s[h]
        d_probs = lax.dot_general(v_s[h, cut, :], d_out, LAST, preferred_element_type=F32)
        d_scores = (exps.astype(F32) * d_probs).astype(BF16)
        probs = (exps.astype(F32) * inverse).astype(BF16)
        d_v = jnp.dot(probs, d_out, preferred_element_type=F32)
        d_k = jnp.dot(d_scores, qs_s[...], preferred_element_type=F32)
        dqt_s[...] += lax.dot_general(k_s[h, cut, :], d_scores, FIRST, preferred_element_type=F32)
        grad_s[h, cut, HEAD_DIM : 2 * HEAD_DIM] = d_k.astype(BF16)
        grad_s[h, cut, 2 * HEAD_DIM : 3 * HEAD_DIM] = d_v[:, 0:HEAD_DIM].astype(BF16)

    def finish(h):
        grad_s[h, :, 0:HEAD_DIM] = (dqt_s[...] * (inv_s[h] * scale)).T.astype(BF16)

    pl.semaphore_wait(barrier, seq + dp - 2)
    w_own(0)
    for g in range(1, heads):
        w_ends(g)
    a_swap().start()
    g_swap().start()
    for copy in loads[:3]:
        copy.wait()
    for h in range(heads):
        pack(h)
        send_all(q_copy, own_q, h)
    for copy in loads[3:]:
        copy.wait()
    for h in range(heads):
        pack_attn(h)
    own_w[0].wait()
    make_d_out(0, d)
    a_swap().wait_recv()
    g_swap().wait_recv()
    p_s[...] = factor * lax.dot_general(
        a2[...].reshape(2 * rows, features), g2[...].reshape(2 * rows, half), FIRST, preferred_element_type=F32
    )
    chain_ends()
    for dist in range(1, dp - 1):
        w_relay(0, dist)
        if dist < dp - 2:
            d_out_pair(0, dist)
    for g in range(1, heads):
        w_inner(g)
    links = [(k, j) for k in range(1, dp - 1) for j in range(PIECES)]

    def link():
        if links:
            chain(*links.pop(0))

    for h in range(heads):
        unpack(h)
        for index in range(blocks):
            soften(h, index)
            if h == 0 and index == 0:
                if dp > 2:
                    d_out_pair(0, dp - 2)
                for g in range(1, heads):
                    own_w[g].wait()
                    make_d_out(g, d)
            if h == 0 and index == blocks - 1:
                w_relay(0, dp - 1)
                d_out_pair(0, dp - 1)
                for g in range(1, heads):
                    if dp > 2:
                        w_relay(g, 1)
                link()
            if h == 1 and index == 0:
                if dp > 2:
                    for g in range(1, heads):
                        d_out_pair(g, 1)
                link()
            if h == 1 and index == blocks - 1:
                for g in range(1, heads):
                    for dist in range(2, dp - 1):
                        w_relay(g, dist)
                        d_out_pair(g, dist)
                link()

    for h in range(heads):
        prepare(h)
        last = h == heads - 1
        for index in range(blocks):
            differentiate(h, index)
            if last and index == blocks - 2:
                while links:
                    link()
                scatter()
        finish(h)
        if h == 0:
            link()
            for g in range(1, heads):
                w_relay(g, dp - 1)
                d_out_pair(g, dp - 1)
        if not last:
            send_all(grad_copy, own_grad, h)
    if blocks == 1:
        while links:
            link()
        scatter()
    own_grad(heads - 1).start()
    for step in range(1, seq):
        grad_copy(heads - 1, lax.rem(s + step, seq), s).start()
        if step == seq - 1:
            combine()
    for step in range(1, chips):
        arrived(lax.rem(s + seq - 2 * step, seq))
        forward(step).start()
    for h in range(heads):
        await_all(grad_copy, own_grad, h)
    for step in range(chips):
        arrived(lax.rem(partner + seq - 2 * step, seq))
    own_total.wait()

    for h in range(heads):
        w_drain(h)
        drain_all(q_copy, h)
        drain_all(do_copy, h)
        drain_all(grad_copy, h)
    a_swap().wait_send()
    g_swap().wait_send()
    chain_drain()
    for step in range(1, chips):
        rs_copy(lax.rem(chip + step, chips), chip).wait_send()
        direct(step).wait_send()
    for step in range(chips):
        forward(step).wait_send()


def attention(seq, dp, factor, query, keys, values, attn, grad_y, w_rows):
    rows, features = query.shape
    heads = w_rows.shape[1]
    ratio = w_rows.shape[0]
    total = seq * rows
    half = features // 2
    slab = features // dp
    chips = seq // 2
    share = slab // chips
    block = 768
    while total % block or total * block > 1536 * 768:
        block //= 2
    dma = pltpu.SemaphoreType.DMA
    hbm = pl.BlockSpec(memory_space=pl.ANY)
    low = lambda *shape: pltpu.VMEM(shape, BF16)
    wide = lambda *shape: pltpu.VMEM(shape, F32)
    links = max(dp - 1, 1)
    return pl.pallas_call(
        functools.partial(attention_kernel, seq, dp, heads, block, factor),
        out_shape=(
            jax.ShapeDtypeStruct((heads, seq, rows, 3 * HEAD_DIM), BF16),
            jax.ShapeDtypeStruct((seq, share, half), BF16),
        ),
        in_specs=[hbm] * 6,
        out_specs=(hbm, hbm),
        scratch_shapes=[
            low(rows, features), low(rows, features), low(rows, features), low(rows, features),
            low(2, rows, features), low(2, rows, half),
            low(heads, seq, HEAD_DIM, features),
            low(heads, seq, rows, 3 * HEAD_DIM), low(heads, seq, rows, 3 * HEAD_DIM),
            low(heads, seq, rows, HEAD_DIM), low(heads, seq, rows // FOLD, FOLD * AUG), low(heads, seq, rows // FOLD, FOLD * AUG),
            low(heads, total, HEAD_DIM), low(heads, total, HEAD_DIM), low(heads, total, AUG),
            low(total, HEAD_DIM), low(total, AUG),
            low(heads, total, total), wide(heads, 1, total),
            wide(HEAD_DIM, total), low(heads, total, 3 * HEAD_DIM),
            wide(features, half),
            *[low(links, PIECES, slab // PIECES, half)] * 4,
            wide(slab, half), low(chips, share, half), low(chips, share, half), low(share, half),
            dma((6 + heads,)), dma((4, heads)),
            dma((heads, dp)), dma((heads, dp)), dma((heads, dp)), dma((heads, dp, 2)),
            dma((2,)), dma((2,)),
            dma((heads, seq)), dma((heads, seq)), dma((heads, seq)), dma((heads, seq)),
            dma((heads, seq)), dma((heads, seq)),
            *[dma((links, PIECES))] * 4,
            dma((chips,)), dma((chips,)), dma((chips,)), dma((chips,)), dma((seq,)),
        ],
        compiler_params=pltpu.CompilerParams(
            collective_id=0, has_side_effects=True, vmem_limit_bytes=VMEM_LIMIT
        ),
        name="attention_backward",
    )(query, keys, values, attn, grad_y, w_rows)


def unpack_kernel(landed, spread, dq_ref, dk_ref, dv_ref, out_ref):
    heads, seq = landed.shape[:2]
    share, half = spread.shape[1:]
    width = heads * HEAD_DIM
    for source in range(seq):
        for h in range(heads):
            start = source * width + h * HEAD_DIM
            for index, ref in enumerate((dq_ref, dk_ref, dv_ref)):
                ref[:, start : start + HEAD_DIM] = landed[
                    h, source, :, index * HEAD_DIM : (index + 1) * HEAD_DIM
                ]
        top = (source // 2) * share
        side = (source % 2) * half
        out_ref[top : top + share, side : side + half] = spread[source].astype(F32)


def unpack(dp, landed, spread):
    rows = landed.shape[2]
    features = landed.shape[0] * landed.shape[1] * HEAD_DIM
    vmem = pl.BlockSpec(memory_space=pltpu.VMEM)
    block = jax.ShapeDtypeStruct((rows, features), BF16)
    return pl.pallas_call(
        unpack_kernel,
        out_shape=(block, block, block, jax.ShapeDtypeStruct((features // dp, features), F32)),
        in_specs=[vmem] * 2,
        out_specs=(vmem,) * 4,
        compiler_params=pltpu.CompilerParams(vmem_limit_bytes=VMEM_LIMIT),
        name="unpack",
    )(landed, spread)


def body(query, keys, values, attn, d_block, w_out):
    seq = lax.axis_size("seq")
    dp = lax.axis_size("dp")
    rows, features = query.shape[1:]
    heads = features // HEAD_DIM // seq
    flat = lambda array: array.reshape(rows, features)
    factor = 1.0 / float(dp * rows * seq) ** 0.5
    landed, spread = attention(
        seq, dp, factor, flat(query), flat(keys), flat(values), flat(attn), flat(d_block),
        w_out.reshape(seq // dp, heads, HEAD_DIM, features),
    )
    d_query, d_keys, d_values, d_weight = unpack(dp, landed, spread)
    whole = lambda array: array.reshape(1, rows, features)
    return whole(d_query), whole(d_keys), whole(d_values), d_weight


def solution(mesh):
    blocks = P("dp", "seq", None)
    return jax.shard_map(
        body,
        mesh=mesh,
        in_specs=(blocks,) * 5 + (P("dp", None),),
        out_specs=(blocks, blocks, blocks, P("dp", None)),
        check_vma=False,
    )
```
